32 devices in a mesh: ax: 8 (over z, y), rad: 4 (over x, core).
Axes of the slice: x: 2, y: 2, z: 4, core: 2. Of those that a mesh axis runs over, the one named last changes fastest.
Arguments:
- face_data: float32 [1024, 7, 5, 128], P('ax', None, None, 'rad'), may hold values from -0.6 to 0.6
- face_station: int32 [1024], P('ax'), may hold values from 0 to 511, as said below
- face_counts: int32 [8], P('ax'), may hold values from 0 to 128, as said below
- mode_slots: int32 [256], replicated, may hold values from 0 to 255, each once
- radial_proj: float32 [32, 128], P(None, 'rad'), may hold values from -0.5 to 0.5
- radial_modes: float32 [64, 32], replicated, may hold values from -1 to 1
- duct_field: float32 [32, 64, 3, 5, 2, 256], P('ax', 'rad'), may hold values from -6 to 6
- mean_mach: float32 [32, 64], P('ax', 'rad'), may hold values from 0.1 to 0.7
- pseudo_step: float32 [32, 64], P('ax', 'rad'), may hold values from 0.06 to 0.2
Outputs:
- duct_next: float32 [32, 64, 3, 5, 2, 256], P('ax', 'rad')
The draws below stay inside these ranges and needn't reach their ends.
Inputs may be any that keep to these rules, and one draw needn't show every extreme that they name: `face_counts`: they sum to 512; one index of ax uses all 128 slots. `face_station`: slot s of ax index a is used when s < face_counts[a] and then names an angular station; each station is named by exactly one used slot; unused slots name arbitrary stations. `mode_slots`: each circumferential mode once.
All inputs are finite; a program needn't handle non-finite values.
Results may differ from the reference program's by a relative error of at most 0.00012.
Values sent between devices are 32-bit elements; how exact they have to be, the bound alone decides.
A program may use at most 128 MiB of HBM per device.

```python
import math
import jax
import jax.numpy as jnp
from jax import lax

NTH = 512
NRF = 128
SAMPLE_MOMENTS = 7
HARM = 3
VARS = 5
NMODE = 256
NRM = 32
NRD = 64
ITERS = 3
CAP = 128
FACE_ROWS = 1024
NX = 32
N_AX = 8


def ragged_layout(key):
    base = jax.random.fold_in(key, 4711)
    key_shift, key_pick, key_sign, key_order, key_filler = jax.random.split(base, 5)
    average = NTH // N_AX
    pair_count = N_AX // 2
    shifts = jax.random.randint(key_shift, (pair_count,), -(average - 1), average)
    selected_pick = jax.random.randint(key_pick, (), 0, pair_count)
    flipper = 2 * jax.random.randint(key_sign, (), 0, 2) - 1
    shifts = jnp.where(jnp.arange(pair_count) == selected_pick, average * flipper, shifts)
    counts = jnp.stack([average + shifts, average - shifts], axis=1).reshape(N_AX).astype(jnp.int32)
    ordering = jax.random.permutation(key_order, NTH).astype(jnp.int32)
    offsets = jnp.cumsum(counts) - counts
    slot_ids = jnp.arange(N_AX * CAP).astype(jnp.int32)
    owner = slot_ids // CAP
    within = slot_ids % CAP
    used = within < counts[owner]
    where_from = jnp.clip(offsets[owner] + within, 0, NTH - 1)
    filler = jax.random.randint(key_filler, (N_AX * CAP,), 0, NTH).astype(jnp.int32)
    stations = jnp.where(used, ordering[where_from], filler).astype(jnp.int32)
    return (counts, stations)


def draw_face_counts(key, part):
    counts, stations = ragged_layout(key)
    return counts


def draw_face_station(key, part):
    counts, stations = ragged_layout(key)
    return stations


def steps_of(key, dims, cuts, low, largest):
    loudness = 1.0
    for axis_at, parts in cuts:
        heights = jax.random.uniform(jax.random.fold_in(jax.random.fold_in(key, 6), axis_at), (parts,), jnp.float32, low / len(cuts), largest / len(cuts))
        loudness = loudness * jnp.repeat(jnp.exp(heights), dims[axis_at] // parts).reshape((-1,) + (1,) * (len(dims) - 1 - axis_at))
    return loudness


def centred(key, extent, deviation, reach, cuts=(), held_as=jnp.bfloat16):
    factor_of = steps_of(key, extent, cuts, -0.22, 0.18) if cuts else 1.0
    drawn = jax.random.normal(key, extent, jnp.float32) * deviation * factor_of
    return jnp.minimum(jnp.maximum(drawn, -reach), reach).astype(held_as)


def setup_inputs(seed: int = 0) -> dict:
    splits = jax.random.split(jax.random.key(seed), 10)
    return {
        "face_data": centred(splits[0], (FACE_ROWS, SAMPLE_MOMENTS, VARS, NRF), 0.1, 0.6, ((0, 8), (3, 4)), jnp.float32),
        "face_station": draw_face_station(jax.random.fold_in(splits[9], 71), 0),
        "face_counts": draw_face_counts(jax.random.fold_in(splits[9], 71), 0),
        "mode_slots": jax.random.permutation(splits[3], NMODE).astype(jnp.int32),
        "radial_proj": centred(splits[4], (NRM, NRF), NRF ** -0.5, 0.5, ((1, 4),), jnp.float32),
        "radial_modes": centred(splits[5], (NRD, NRM), NRM ** -0.5, 1.0, (), jnp.float32),
        "duct_field": centred(splits[6], (NX, NRD, HARM, VARS, 2, NMODE), 1.0, 6.0, ((0, 8), (1, 4)), jnp.float32),
        "mean_mach": jnp.clip(0.1 + 0.59999999 * jax.random.uniform(splits[7], (NX, NRD), jnp.float32) ** steps_of(splits[7], (NX, NRD), ((0, 8), (1, 4)), -0.2, 0.2), 0.1, 0.7),
        "pseudo_step": jnp.clip(0.06 + 0.14 * jax.random.uniform(splits[8], (NX, NRD), jnp.float32) ** steps_of(splits[8], (NX, NRD), ((0, 8), (1, 4)), -0.2, 0.2), 0.06, 0.2),
    }


OMEGA_STEP = 0.35
DAMPING = 0.25


def rotate(part):
    return jnp.stack([-part[..., 1, :], part[..., 0, :]], axis=-2)


def advance(padded, mach, step_size, inv_radius, modes):
    centre = padded[1:-1, 1:-1]
    along = (padded[2:, 1:-1] - padded[:-2, 1:-1]) * 0.5
    across = (padded[1:-1, 2:] - padded[1:-1, :-2]) * 0.5
    damped_filter = padded[2:, 1:-1] + padded[:-2, 1:-1] + padded[1:-1, 2:] + padded[1:-1, :-2] - 4.0 * centre
    frequency_order = jnp.arange(1, HARM + 1).astype(jnp.float32)
    omega = (OMEGA_STEP * frequency_order)[:, None, None]
    mach_cell = mach[:, :, None, None, None]
    radius_cell = inv_radius[None, :, None, None, None]
    density = centre[:, :, :, 0]
    axial = centre[:, :, :, 1]
    radial = centre[:, :, :, 2]
    swirl = centre[:, :, :, 3]
    pressure = centre[:, :, :, 4]
    source = along[:, :, :, 1] + across[:, :, :, 2] + radial * radius_cell + rotate(swirl) * modes * radius_cell
    res_density = omega * rotate(density) + mach_cell * along[:, :, :, 0] + source
    res_axial = omega * rotate(axial) + mach_cell * along[:, :, :, 1] + along[:, :, :, 4]
    res_radial = omega * rotate(radial) + mach_cell * along[:, :, :, 2] + across[:, :, :, 4]
    res_swirl = omega * rotate(swirl) + mach_cell * along[:, :, :, 3] + rotate(pressure) * modes * radius_cell
    res_pressure = omega * rotate(pressure) + mach_cell * along[:, :, :, 4] + source
    residual = jnp.stack([res_density, res_axial, res_radial, res_swirl, res_pressure], axis=3)
    step_cell = step_size[:, :, None, None, None, None]
    return centre - step_cell * (residual - DAMPING * damped_filter)


def project(face_data, face_station, valid, wave_orders, radial_proj):
    frequency_order = jnp.arange(1, HARM + 1).astype(jnp.int32)
    sample_moments = jnp.arange(SAMPLE_MOMENTS).astype(jnp.int32)
    revolution_count = ((frequency_order[:, None] * sample_moments[None, :]) % SAMPLE_MOMENTS).astype(jnp.float32) * (2.0 * math.pi / SAMPLE_MOMENTS)
    twiddle = jnp.stack([jnp.cos(revolution_count), -jnp.sin(revolution_count)], axis=1) * (2.0 / SAMPLE_MOMENTS)
    spectral_values = jnp.einsum('rtvj,kct->rkvcj', face_data, twiddle, precision=lax.Precision.HIGHEST)
    phase = jnp.mod(face_station[:, None] * wave_orders[None, :], NTH).astype(jnp.float32) * (2.0 * math.pi / NTH)
    cosine = jnp.where(valid[:, None], jnp.cos(phase), 0.0)
    sine = jnp.where(valid[:, None], jnp.sin(phase), 0.0)
    with_cos = jnp.einsum('rs,rkvcj->kvcjs', cosine, spectral_values, precision=lax.Precision.HIGHEST)
    with_sin = jnp.einsum('rs,rkvcj->kvcjs', sine, spectral_values, precision=lax.Precision.HIGHEST)
    real_part = with_cos[:, :, 0] + with_sin[:, :, 1]
    imag_part = with_cos[:, :, 1] - with_sin[:, :, 0]
    fourier_transform = jnp.stack([real_part, imag_part], axis=2)
    return jnp.einsum('nj,kvcjs->nkvcs', radial_proj, fourier_transform, precision=lax.Precision.HIGHEST)


def reference(face_data, face_station, face_counts, mode_slots, radial_proj, radial_modes, duct_field, mean_mach, pseudo_step):
    rows = jnp.arange(FACE_ROWS).astype(jnp.int32)
    valid = (rows % CAP) < face_counts[rows // CAP]
    wave_orders = (mode_slots - NMODE // 2).astype(jnp.int32)
    modal_amplitudes = project(face_data, face_station, valid, wave_orders, radial_proj)
    boundary = jnp.einsum('jn,nkvcs->jkvcs', radial_modes, modal_amplitudes, precision=lax.Precision.HIGHEST)
    inv_radius = 1.0 / (NRD + jnp.arange(NRD).astype(jnp.float32) + 0.5)
    modes = wave_orders.astype(jnp.float32)
    block = math.gcd(NMODE, 32)
    blocks = NMODE // block
    fields = jnp.moveaxis(duct_field.reshape(NX, NRD, HARM, VARS, 2, blocks, block), 5, 0)
    bounds = jnp.moveaxis(boundary.reshape(NRD, HARM, VARS, 2, blocks, block), 4, 0)
    mode_blocks = modes.reshape(blocks, block)

    def run_block(pieces):
        field, bound, mode_values = pieces
        for sweep in range(ITERS):
            padded = jnp.pad(field, ((1, 1), (1, 1), (0, 0), (0, 0), (0, 0), (0, 0)))
            padded = padded.at[0, 1:-1].set(bound)
            field = advance(padded, mean_mach, pseudo_step, inv_radius, mode_values)
        return field

    result = lax.map(run_block, (fields, bounds, mode_blocks))
    return jnp.moveaxis(result, 0, 5).reshape(NX, NRD, HARM, VARS, 2, NMODE)
```

```python
import functools
import math

import jax
import jax.numpy as jnp
from jax import lax
from jax.experimental import pallas as pl
from jax.experimental.pallas import tpu as pltpu
from jax.sharding import PartitionSpec as P

NTH = 512
SAMPLE_MOMENTS = 7
HARM = 3
NMODE = 256
NRM = 32
NRD = 64
ITERS = 3
VARS = 5

OMEGA_STEP = 0.35
DAMPING = 0.25

MESH = pl.DeviceIdType.MESH
GROUP = VARS * 2 * 2
PLANES = HARM * GROUP
PAD = 8


def dot_nt(a, b):
    return lax.dot_general(
        a, b, (((1,), (1,)), ((), ())),
        precision=lax.Precision.HIGHEST, preferred_element_type=jnp.float32,
    )


def dot_nn(a, b):
    return lax.dot_general(
        a, b, (((1,), (0,)), ((), ())),
        precision=lax.Precision.HIGHEST, preferred_element_type=jnp.float32,
    )


def kernel(
    n_ax, n_rad, layers, rows,
    x_hbm, face, weights, cosine, sine, shapes, mach, step, invr, mode_r,
    out,
    T, part, a_recv, total, c_recv, b_recv, bound,
    load_sem, ax_send, ax_recv, rad_send, rad_recv, late_send, late_recv,
    a_send, a_sem, c_send, c_sem, b_send, b_sem, d_send, d_sem,
):
    ax = lax.axis_index("ax")
    rad = lax.axis_index("rad")
    share = PLANES // n_rad
    own = pl.ds(PAD, rows)
    peers_c = n_ax // 2 - 1
    top = layers + 1

    barrier = pltpu.get_barrier_semaphore()

    def greet(**where):
        pl.semaphore_signal(barrier, inc=1, device_id=where, device_id_type=MESH)

    pl.when(ax > 0)(lambda: greet(ax=ax - 1))
    pl.when(ax < n_ax - 1)(lambda: greet(ax=ax + 1))
    for d in range(1, n_rad):
        greet(rad=lax.rem(rad + d, n_rad))
    pl.when(ax >= 2)(lambda: greet(ax=lax.rem(ax, 2)))

    @pl.when(ax < 2)
    def _():
        for i in range(peers_c):
            greet(ax=ax + 2 * (i + 1))

    count = (
        jnp.where(ax > 0, 1, 0) + jnp.where(ax < n_ax - 1, 1, 0) + (n_rad - 1)
        + jnp.where(ax >= 2, 1, peers_c)
    )
    pl.semaphore_wait(barrier, count)

    def group(k):
        return pl.ds(k * GROUP, GROUP)

    def axial(t, k, side):
        source_layer = layers if side == 0 else 1
        if t == 0:
            src = x_hbm.at[source_layer - 1, group(k)]
        else:
            src = T.at[t, source_layer, group(k), own]
        return pltpu.make_async_remote_copy(
            src_ref=src,
            dst_ref=T.at[t, 0 if side == 0 else top, group(k), own],
            send_sem=ax_send.at[t, k, side],
            recv_sem=ax_recv.at[t, k, side],
            device_id={"ax": ax + 1 if side == 0 else ax - 1},
            device_id_type=MESH,
        )

    def radial(t, k, side, lo, hi, late=False):
        count_l = hi - lo
        first = rows - PAD if side == 0 else 0
        if t == 0:
            src = x_hbm.at[pl.ds(lo - 1, count_l), group(k), pl.ds(first, PAD)]
        else:
            src = T.at[t, pl.ds(lo, count_l), group(k), pl.ds(PAD + first, PAD)]
        send, recv = (late_send, late_recv) if late else (rad_send, rad_recv)
        return pltpu.make_async_remote_copy(
            src_ref=src,
            dst_ref=T.at[
                t, pl.ds(lo, count_l), group(k), pl.ds(0 if side == 0 else PAD + rows, PAD)
            ],
            send_sem=send.at[t, k, side],
            recv_sem=recv.at[t, k, side],
            device_id={"rad": rad + 1 if side == 0 else rad - 1},
            device_id_type=MESH,
        )

    can_send = {
        ("ax", 0): ax < n_ax - 1, ("ax", 1): ax > 0,
        ("rad", 0): rad < n_rad - 1, ("rad", 1): rad > 0,
    }
    can_recv = {
        ("ax", 0): ax > 0, ("ax", 1): ax < n_ax - 1,
        ("rad", 0): rad > 0, ("rad", 1): rad < n_rad - 1,
    }

    def axial_all(t, k, what):
        table = can_recv if what == "wait_recv" else can_send
        for side in (0, 1):
            pl.when(table["ax", side])(
                lambda side=side: getattr(axial(t, k, side), what)()
            )

    def radial_all(t, k, what):
        table = can_recv if what == "wait_recv" else can_send
        for side in (0, 1):
            if t == 0:
                pl.when(table["rad", side])(
                    lambda side=side: getattr(radial(0, k, side, 1, top), what)()
                )
            else:
                pl.when(table["rad", side] & (ax > 0))(
                    lambda side=side: getattr(radial(t, k, side, 1, top), what)()
                )
                pl.when(table["rad", side] & (ax == 0))(
                    lambda side=side: getattr(radial(t, k, side, t + 1, top), what)()
                )

    def radial_late(t, k, what):
        table = can_recv if what == "wait_recv" else can_send
        for side in (0, 1):
            pl.when(table["rad", side])(
                lambda side=side: getattr(radial(t, k, side, 1, t + 1, True), what)()
            )

    for k in range(HARM):
        axial_all(0, k, "start")
        radial_all(0, k, "start")
    load = pltpu.make_async_copy(
        x_hbm, T.at[0, pl.ds(1, layers), :, own], load_sem
    )
    load.start()

    zero_rows = jnp.zeros((PAD, 128), jnp.float32)

    @pl.when(ax == n_ax - 1)
    def _():
        @pl.loop(0, PLANES)
        def _(q):
            for t in range(ITERS):
                T[t, top, q, own, :] = jnp.zeros((rows, 128), jnp.float32)

    for edge, start in ((rad == 0, 0), (rad == n_rad - 1, PAD + rows)):
        @pl.when(edge)
        def _(start=start):
            @pl.loop(0, PLANES)
            def _(q):
                for t in range(ITERS):
                    for l in range(1, top):
                        T[t, l, q, pl.ds(start, PAD), :] = zero_rows

    slots = face.shape[1]
    for v in range(VARS):
        spectra = dot_nt(weights[...], face[v])
        half = HARM * NRM
        y0, y1 = spectra[:half], spectra[half:]
        real = dot_nn(y0, cosine[...]) + dot_nn(y1, sine[...])
        imag = dot_nn(y1, cosine[...]) - dot_nn(y0, sine[...])
        for c, value in ((0, real), (1, imag)):
            for k in range(HARM):
                for sh in range(2):
                    part[k * GROUP + v * 4 + c * 2 + sh] = value[
                        k * NRM:(k + 1) * NRM, sh * 128:(sh + 1) * 128
                    ]

    def scatter(d):
        peer = lax.rem(rad + d, n_rad)
        return pltpu.make_async_remote_copy(
            src_ref=part.at[pl.ds(peer * share, share)],
            dst_ref=a_recv.at[d - 1],
            send_sem=a_send.at[d - 1],
            recv_sem=a_sem.at[d - 1],
            device_id={"rad": peer},
            device_id_type=MESH,
        )

    for d in range(1, n_rad):
        scatter(d).start()
    for d in range(1, n_rad):
        scatter(d).wait_recv()

    @pl.loop(0, share)
    def _(q):
        acc = part[rad * share + q]
        for d in range(n_rad - 1):
            acc = acc + a_recv[d, q]
        total[0, q] = acc

    def to_front():
        return pltpu.make_async_remote_copy(
            src_ref=total.at[0],
            dst_ref=c_recv.at[ax // 2 - 1],
            send_sem=c_send,
            recv_sem=c_sem.at[ax // 2 - 1],
            device_id={"ax": lax.rem(ax, 2)},
            device_id_type=MESH,
        )

    def to_inlet():
        return pltpu.make_async_remote_copy(
            src_ref=total.at[1],
            dst_ref=b_recv,
            send_sem=b_send,
            recv_sem=b_sem,
            device_id={"ax": 0},
            device_id_type=MESH,
        )

    def hand_out(d):
        peer = lax.rem(rad + d, n_rad)
        return pltpu.make_async_remote_copy(
            src_ref=bound.at[peer],
            dst_ref=T.at[0, 0, pl.ds(rad * share, share), own],
            send_sem=d_send.at[d - 1],
            recv_sem=d_sem.at[d - 1],
            device_id={"rad": peer},
            device_id_type=MESH,
        )

    def gather_front():
        for i in range(peers_c):
            pltpu.make_async_copy(c_recv.at[i], c_recv.at[i], c_sem.at[i]).wait()

        @pl.loop(0, share)
        def _(q):
            acc = total[0, q]
            for i in range(peers_c):
                acc = acc + c_recv[i, q]
            total[1, q] = acc

    pl.when(ax >= 2)(lambda: to_front().start())
    load.wait()

    def update(t, k, lo, hi):
        omega = OMEGA_STEP * (k + 1).astype(jnp.float32)

        def layer_body(i, carry):
            l = lo + i // 2
            sh = lax.rem(i, 2)
            for h in range(rows // 8):
                r0 = PAD + 8 * h
                here = pl.ds(8 * h, 8)
                m = mach[l - 1, here, :]
                dt = step[l - 1, here, :]
                ir = invr[here, :]
                mr = mode_r[sh, here, :]
                base = k * GROUP + sh

                def get(v, c, dl=0, dr=0):
                    return T[t, l + dl, base + v * 4 + c * 2, pl.ds(r0 + dr, 8), :]

                centre = [[get(v, c) for c in (0, 1)] for v in range(VARS)]

                def rot(v, c):
                    return -centre[v][1] if c == 0 else centre[v][0]

                def diff(v, c):
                    up, dn = get(v, c, 1), get(v, c, -1)
                    rt, lf = get(v, c, 0, 1), get(v, c, 0, -1)
                    along = (up - dn) * 0.5
                    across = (rt - lf) * 0.5
                    return along, across, (up + dn) + (rt + lf) - 4.0 * centre[v][c]

                for c in (0, 1):
                    d = [diff(v, c) for v in range(VARS)]
                    source = d[1][0] + d[2][1] + centre[2][c] * ir + rot(3, c) * mr
                    extra = [source, d[4][0], d[4][1], rot(4, c) * mr, source]
                    for v in range(VARS):
                        residual = omega * rot(v, c) + m * d[v][0] + extra[v]
                        value = centre[v][c] - dt * (residual - DAMPING * d[v][2])
                        q = base + v * 4 + c * 2
                        if t == ITERS - 1:
                            out[l - 1, q, here, :] = value
                        else:
                            T[t + 1, l, q, pl.ds(r0, 8), :] = value
            return carry

        lax.fori_loop(0, 2 * (hi - lo), layer_body, 0)

    def early(t):
        @pl.loop(0, HARM)
        def _(k):
            radial_all(t, k, "wait_recv")
            axial_all(t, k, "wait_recv")
            update(t, k, jnp.where(ax == 0, t + 2, 1), top)
            if t < ITERS - 1:
                axial_up_down(t + 1, k)
                radial_all(t + 1, k, "start")

    def axial_up_down(t, k):
        axial_all(t, k, "start")

    def late(t):
        @pl.loop(0, HARM)
        def _(k):
            if t > 0:
                radial_late(t, k, "wait_recv")
            update(t, k, 1, t + 2)
            if t < ITERS - 1:
                radial_late(t + 1, k, "start")

    early(0)

    @pl.when(ax < 2)
    def _():
        gather_front()

    pl.when(ax == 1)(lambda: to_inlet().start())
    early(1)

    @pl.when(ax == 0)
    def _():
        to_inlet_wait = pltpu.make_async_copy(b_recv, b_recv, b_sem)
        to_inlet_wait.wait()

        @pl.loop(0, share)
        def _(q):
            value = dot_nn(shapes[...], total[1, q] + b_recv[q])
            for r in range(n_rad):
                bound[r, q] = value[r * rows:(r + 1) * rows]

        for d in range(1, n_rad):
            hand_out(d).start()

        @pl.loop(0, share)
        def _(q):
            T[0, 0, rad * share + q, own, :] = bound[rad, q]

        for d in range(1, n_rad):
            src = lax.rem(rad + n_rad - d, n_rad)
            place = T.at[0, 0, pl.ds(src * share, share), own]
            pltpu.make_async_copy(place, place, d_sem.at[d - 1]).wait()

        @pl.loop(0, PLANES)
        def _(q):
            value = T[0, 0, q, own, :]
            for t in range(1, ITERS):
                T[t, 0, q, own, :] = value

        late(0)
        late(1)

    early(2)
    pl.when(ax == 0)(lambda: late(2))

    for t in range(ITERS):
        @pl.loop(0, HARM)
        def _(k):
            axial_all(t, k, "wait_send")
            radial_all(t, k, "wait_send")
            if t > 0:
                pl.when(ax == 0)(lambda: radial_late(t, k, "wait_send"))
    for d in range(1, n_rad):
        scatter(d).wait_send()
    pl.when(ax >= 2)(lambda: to_front().wait_send())
    pl.when(ax == 1)(lambda: to_inlet().wait_send())

    @pl.when(ax == 0)
    def _():
        for d in range(1, n_rad):
            hand_out(d).wait_send()


def on_device(
    n_ax, n_rad,
    face_data, face_station, face_counts, mode_slots, radial_proj, radial_modes,
    duct_field, mean_mach, pseudo_step,
):
    layers, rows = duct_field.shape[:2]
    slots = face_station.shape[0]
    valid = jnp.arange(slots) < face_counts[0]
    orders = mode_slots - NMODE // 2
    frequency_order = jnp.arange(1, HARM + 1)
    moments = jnp.arange(SAMPLE_MOMENTS)
    turns = (frequency_order[:, None] * moments[None, :] % SAMPLE_MOMENTS).astype(
        jnp.float32
    ) * (2.0 * math.pi / SAMPLE_MOMENTS)
    twiddle = jnp.stack([jnp.cos(turns), -jnp.sin(turns)], axis=0) * (2.0 / SAMPLE_MOMENTS)
    width = face_data.shape[3]
    weights = (
        twiddle[:, :, None, :, None] * radial_proj[None, None, :, None, :]
    ).reshape(2 * HARM * NRM, SAMPLE_MOMENTS * width)
    face = jnp.transpose(face_data, (2, 0, 1, 3)).reshape(VARS, slots, SAMPLE_MOMENTS * width)
    phase = jnp.mod(face_station[:, None] * orders[None, :], NTH).astype(jnp.float32) * (
        2.0 * math.pi / NTH
    )
    cosine = jnp.where(valid[:, None], jnp.cos(phase), 0.0)
    sine = jnp.where(valid[:, None], jnp.sin(phase), 0.0)

    radial_start = lax.axis_index("rad") * rows
    global_rows = (radial_start + jnp.arange(rows)).astype(jnp.float32)
    inv_radius = 1.0 / (NRD + global_rows + 0.5)
    modes = orders.astype(jnp.float32).reshape(2, 1, 128)
    invr = jnp.broadcast_to(inv_radius[:, None], (rows, 128))
    mode_r = modes * inv_radius[None, :, None]
    mach = jnp.broadcast_to(mean_mach[:, :, None], (layers, rows, 128))
    step = jnp.broadcast_to(pseudo_step[:, :, None], (layers, rows, 128))
    x = jnp.transpose(
        duct_field.reshape(layers, rows, PLANES // 2, 2, 128), (0, 2, 3, 1, 4)
    ).reshape(layers, PLANES, rows, 128)

    share = PLANES // n_rad
    vmem = pl.BlockSpec(memory_space=pltpu.VMEM)
    dma = pltpu.SemaphoreType.DMA
    out = pl.pallas_call(
        functools.partial(kernel, n_ax, n_rad, layers, rows),
        out_shape=jax.ShapeDtypeStruct((layers, PLANES, rows, 128), jnp.float32),
        in_specs=[pl.BlockSpec(memory_space=pl.ANY)] + [vmem] * 9,
        out_specs=vmem,
        scratch_shapes=[
            pltpu.VMEM((ITERS, layers + 2, PLANES, rows + 2 * PAD, 128), jnp.float32),
            pltpu.VMEM((PLANES, NRM, 128), jnp.float32),
            pltpu.VMEM((n_rad - 1, share, NRM, 128), jnp.float32),
            pltpu.VMEM((2, share, NRM, 128), jnp.float32),
            pltpu.VMEM((n_ax // 2 - 1, share, NRM, 128), jnp.float32),
            pltpu.VMEM((share, NRM, 128), jnp.float32),
            pltpu.VMEM((n_rad, share, rows, 128), jnp.float32),
            dma,
            dma((ITERS, HARM, 2)), dma((ITERS, HARM, 2)),
            dma((ITERS, HARM, 2)), dma((ITERS, HARM, 2)),
            dma((ITERS, HARM, 2)), dma((ITERS, HARM, 2)),
            dma((n_rad - 1,)), dma((n_rad - 1,)),
            dma, dma((n_ax // 2 - 1,)),
            dma, dma,
            dma((n_rad - 1,)), dma((n_rad - 1,)),
        ],
        compiler_params=pltpu.CompilerParams(
            collective_id=0, has_side_effects=True, vmem_limit_bytes=60 * 1024 * 1024
        ),
    )(x, face, weights, cosine, sine, radial_modes, mach, step, invr, mode_r)
    return jnp.transpose(
        out.reshape(layers, PLANES // 2, 2, rows, 128), (0, 3, 1, 2, 4)
    ).reshape(duct_field.shape)


def solution(mesh):
    in_specs = (
        P("ax", None, None, "rad"),
        P("ax"),
        P("ax"),
        P(),
        P(None, "rad"),
        P(),
        P("ax", "rad", None, None, None, None),
        P("ax", "rad"),
        P("ax", "rad"),
    )
    out_specs = P("ax", "rad", None, None, None, None)
    return jax.shard_map(
        functools.partial(on_device, mesh.shape["ax"], mesh.shape["rad"]),
        mesh=mesh, in_specs=in_specs, out_specs=out_specs, check_vma=False,
    )
```

```python
import functools
import math

import jax
import jax.numpy as jnp
from jax import lax
from jax.experimental import pallas as pl
from jax.experimental.pallas import tpu as pltpu
from jax.sharding import PartitionSpec as P

NTH = 512
SAMPLE_MOMENTS = 7
HARM = 3
NMODE = 256
NRM = 32
NRD = 64
ITERS = 3
VARS = 5

OMEGA_STEP = 0.35
DAMPING = 0.25

MESH = pl.DeviceIdType.MESH
GROUP = VARS * 2
PLANES = HARM * GROUP
PAD = 8
HALF = 128
SLOTS = 32
STEPS = (
    (0, 0), (0, 1), (1, 0), (2, 0), (0, 2), (1, 1),
    (3, 0), (2, 1), (1, 2), (3, 1), (2, 2), (3, 2),
)


def dot_nn(a, b):
    return lax.dot_general(
        a, b, (((1,), (0,)), ((), ())),
        precision=lax.Precision.HIGHEST, preferred_element_type=jnp.float32,
    )


def kernel(
    n_ax, n_rad, layers, rows,
    x_hbm, face, weights, cosine, sine, shapes, coef_in, invr, mode_r,
    out,
    T, coef, part, a_recv, total, y_recv, merged, c_recv, bound, ghost,
    load_sem, out_sem, coef_load, coef_send, coef_recv,
    in_send, in_recv, back_send, back_recv,
    z_send, z_recv, rad_send, rad_recv, late_send, late_recv,
    a_send, a_sem, y_send, y_sem, c_send, c_sem, d_send, d_sem,
):
    ax = lax.axis_index("ax")
    rad = lax.axis_index("rad")
    side_y = lax.rem(ax, 2)
    pair = ax // 2
    mate = ax + 1 - 2 * side_y
    pairs = n_ax // 2
    deep = 2 * layers
    top = deep + 1
    own = pl.ds(PAD, rows)
    share = 2 * SLOTS // n_rad
    half_share = share // 2
    mine = 1 + side_y * layers
    theirs = 1 + (1 - side_y) * layers
    my_lanes = pl.ds(pl.multiple_of(side_y * HALF, HALF), HALF)
    their_lanes = pl.ds(pl.multiple_of((1 - side_y) * HALF, HALF), HALF)
    front = pair == 0
    per_half = n_rad // 2
    half_of = rad // per_half

    barrier = pltpu.get_barrier_semaphore()

    def greet(**where):
        pl.semaphore_signal(barrier, inc=1, device_id=where, device_id_type=MESH)

    greet(ax=mate)
    for d in range(1, n_rad):
        greet(rad=lax.rem(rad + d, n_rad))

    @pl.when(front)
    def _():
        for i in range(1, pairs):
            greet(ax=ax + 2 * i)
        for d in range(1, n_rad):
            pl.semaphore_signal(
                barrier, inc=1,
                device_id=(mate, lax.rem(rad + d, n_rad)), device_id_type=MESH,
            )

    @pl.when(pair > 0)
    def _():
        greet(ax=side_y)

    @pl.when(pair > 1)
    def _():
        greet(ax=ax - 2)

    @pl.when((pair > 0) & (pair < pairs - 1))
    def _():
        greet(ax=ax + 2)

    count = (
        1 + (n_rad - 1)
        + jnp.where(front, pairs - 1 + n_rad - 1, 1)
        + jnp.where(pair > 1, 1, 0)
        + jnp.where((pair > 0) & (pair < pairs - 1), 1, 0)
    )
    pl.semaphore_wait(barrier, count)

    def group(k):
        return pl.ds(k * GROUP, GROUP)

    def remote(src, dst, send, recv, **where):
        return pltpu.make_async_remote_copy(
            src_ref=src, dst_ref=dst, send_sem=send, recv_sem=recv,
            device_id=where, device_id_type=MESH,
        )

    def arrived(ref, sem):
        pltpu.make_async_copy(ref, ref, sem).wait()

    def fetch(k):
        return remote(
            x_hbm.at[:, group(k), :, their_lanes],
            T.at[0, pl.ds(mine, layers), group(k), own],
            in_send.at[k], in_recv.at[k], ax=mate,
        )

    def fetched(k):
        arrived(T.at[0, pl.ds(theirs, layers), group(k), own], in_recv.at[k])

    def give_back(k):
        return remote(
            T.at[ITERS, pl.ds(theirs, layers), group(k), own],
            out.at[:, group(k), :, my_lanes],
            back_send.at[k], back_recv.at[k], ax=mate,
        )

    def given(k):
        arrived(out.at[:, group(k), :, their_lanes], back_recv.at[k])

    def along_z(t, k, side):
        return remote(
            T.at[t, deep if side == 0 else 1, group(k), own],
            T.at[t, 0 if side == 0 else top, group(k), own],
            z_send.at[t, k, side], z_recv.at[t, k, side],
            ax=ax + 2 if side == 0 else ax - 2,
        )

    def radial(t, k, side, lo, count_l, late=False):
        first = rows - PAD if side == 0 else 0
        send, recv = (late_send, late_recv) if late else (rad_send, rad_recv)
        return remote(
            T.at[t, pl.ds(lo, count_l), group(k), pl.ds(PAD + first, PAD)],
            T.at[
                t, pl.ds(lo, count_l), group(k), pl.ds(0 if side == 0 else PAD + rows, PAD)
            ],
            send.at[t, k, side], recv.at[t, k, side],
            rad=rad + 1 if side == 0 else rad - 1,
        )

    can_send = {
        ("z", 0): pair < pairs - 1, ("z", 1): pair > 0,
        ("rad", 0): rad < n_rad - 1, ("rad", 1): rad > 0,
    }
    can_recv = {
        ("z", 0): pair > 0, ("z", 1): pair < pairs - 1,
        ("rad", 0): rad > 0, ("rad", 1): rad < n_rad - 1,
    }

    def z_all(t, k, what):
        table = can_recv if what == "wait_recv" else can_send
        for side in (0, 1):
            pl.when(table["z", side])(
                lambda side=side: getattr(along_z(t, k, side), what)()
            )

    def radial_all(t, k, what):
        table = can_recv if what == "wait_recv" else can_send
        for side in (0, 1):
            pl.when(table["rad", side] & ((pair > 0) | (t == 0)))(
                lambda side=side: getattr(radial(t, k, side, 1, deep), what)()
            )
            for s in range(1, ITERS):
                pl.when(table["rad", side] & front & (t == s))(
                    lambda side=side, s=s: getattr(radial(s, k, side, s + 1, deep - s), what)()
                )

    def radial_late(t, k, what):
        table = can_recv if what == "wait_recv" else can_send
        for side in (0, 1):
            for s in range(1, ITERS):
                pl.when(table["rad", side] & (t == s))(
                    lambda side=side, s=s: getattr(radial(s, k, side, 1, s, True), what)()
                )

    def give_coef():
        return remote(coef_in, coef.at[:, pl.ds(mine, layers)], coef_send, coef_recv, ax=mate)

    fetch(0).start()
    give_coef().start()
    for k in range(1, HARM):
        fetch(k).start()
    load = pltpu.make_async_copy(
        x_hbm.at[:, :, :, my_lanes], T.at[0, pl.ds(mine, layers), :, own], load_sem
    )
    load.start()
    keep_coef = pltpu.make_async_copy(coef_in, coef.at[:, pl.ds(mine, layers)], coef_load)
    keep_coef.start()

    zero_rows = jnp.zeros((PAD, 128), jnp.float32)

    @pl.when(pair == pairs - 1)
    def _():
        @pl.loop(0, PLANES)
        def _(q):
            for t in range(ITERS):
                T[t, top, q, own, :] = jnp.zeros((rows, 128), jnp.float32)

    for edge, start in ((rad == 0, 0), (rad == n_rad - 1, PAD + rows)):
        @pl.when(edge)
        def _(start=start):
            @pl.loop(0, PLANES)
            def _(q):
                for t in range(ITERS):
                    for l in range(1, top):
                        T[t, l, q, pl.ds(start, PAD), :] = zero_rows

    for sh in range(2):
        for q in range(PLANES, SLOTS):
            part[sh * SLOTS + q] = jnp.zeros((NRM, HALF), jnp.float32)
    for v in range(VARS):
        spectra = dot_nn(
            weights[...], jnp.concatenate([face[t, v] for t in range(SAMPLE_MOMENTS)], axis=0)
        )
        half = HARM * NRM
        y0, y1 = spectra[:half], spectra[half:]
        real = dot_nn(y0, cosine[...]) + dot_nn(y1, sine[...])
        imag = dot_nn(y1, cosine[...]) - dot_nn(y0, sine[...])
        for c, value in ((0, real), (1, imag)):
            for k in range(HARM):
                for sh in range(2):
                    part[sh * SLOTS + k * GROUP + v * 2 + c] = value[
                        k * NRM:(k + 1) * NRM, sh * HALF:(sh + 1) * HALF
                    ]

    def scatter(d):
        peer = lax.rem(rad + d, n_rad)
        return remote(
            part.at[pl.ds(peer * share, share)], a_recv.at[d - 1],
            a_send.at[d - 1], a_sem.at[d - 1], rad=peer,
        )

    for d in range(1, n_rad):
        scatter(d).start()

    load.wait()
    keep_coef.wait()

    def keep(kk):
        return pltpu.make_async_copy(
            T.at[ITERS, pl.ds(mine, layers), group(kk), own],
            out.at[:, group(kk), :, my_lanes],
            out_sem.at[kk],
        )

    def to_mate():
        return remote(
            total.at[pl.ds((1 - side_y) * half_share, half_share)], y_recv,
            y_send, y_sem, ax=mate,
        )

    def to_front():
        return remote(merged.at[0], c_recv.at[pair - 1], c_send, c_sem.at[pair - 1], ax=side_y)

    inside = half_of == side_y
    place = lax.rem(rad, per_half)

    def hand_out(r):
        return pltpu.make_async_remote_copy(
            src_ref=bound.at[r],
            dst_ref=ghost.at[pl.ds(place * share + side_y * half_share, half_share)],
            send_sem=d_send.at[r],
            recv_sem=d_sem.at[place * 2 + side_y],
            device_id=(half_of, r),
            device_id_type=MESH,
        )

    def hand_out_all(what):
        for r in range(n_rad):
            pl.when(jnp.logical_not(inside & (rad == r)))(
                lambda r=r: getattr(hand_out(r), what)()
            )

    def sum_rad():
        for d in range(1, n_rad):
            scatter(d).wait_recv()

        @pl.loop(0, share)
        def _(q):
            acc = part[rad * share + q]
            for d in range(n_rad - 1):
                acc = acc + a_recv[d, q]
            total[q] = acc

        to_mate().start()

    def sum_pair():
        arrived(y_recv, y_sem)

        @pl.loop(0, half_share)
        def _(q):
            merged[0, q] = total[side_y * half_share + q] + y_recv[q]

        pl.when(pair > 0)(lambda: to_front().start())

    def inlet():
        for i in range(pairs - 1):
            arrived(c_recv.at[i], c_sem.at[i])

        @pl.loop(0, half_share)
        def _(q):
            acc = merged[0, q]
            for i in range(pairs - 1):
                acc = acc + c_recv[i, q]
            value = dot_nn(shapes[...], acc)
            for r in range(n_rad):
                bound[r, q] = value[r * rows:(r + 1) * rows]

        hand_out_all("start")

        @pl.when(inside)
        def _():
            @pl.loop(0, half_share)
            def _(q):
                ghost[place * share + side_y * half_share + q] = bound[rad, q]

    def inlet_arrived():
        for i in range(per_half):
            for sy in range(2):
                pl.when(jnp.logical_not(inside & (place == i) & (side_y == sy)))(
                    lambda i=i, sy=sy: arrived(
                        ghost.at[pl.ds(i * share + sy * half_share, half_share)],
                        d_sem.at[i * 2 + sy],
                    )
                )

        @pl.loop(0, PLANES)
        def _(q):
            value = ghost[q]
            for t in range(ITERS):
                T[t, 0, q, own, :] = value

    def update(t, k, lo, hi):
        omega = OMEGA_STEP * (k + 1).astype(jnp.float32)
        base = k * GROUP

        def layer_body(l, carry):
            for h in range(rows // 8):
                r0 = PAD + 8 * h
                here = pl.ds(8 * h, 8)
                m = coef[0, l, here, :]
                dt = coef[1, l, here, :]
                ir = invr[here, :]
                mr = mode_r[side_y, here, :]

                def get(v, c, dl=0, dr=0):
                    return T[t, l + dl, base + v * 2 + c, pl.ds(r0 + dr, 8), :]

                centre = [[get(v, c) for c in (0, 1)] for v in range(VARS)]

                def rot(v, c):
                    return -centre[v][1] if c == 0 else centre[v][0]

                def diff(v, c):
                    up, dn = get(v, c, 1), get(v, c, -1)
                    rt, lf = get(v, c, 0, 1), get(v, c, 0, -1)
                    along = (up - dn) * 0.5
                    across = (rt - lf) * 0.5
                    return along, across, (up + dn) + (rt + lf) - 4.0 * centre[v][c]

                for c in (0, 1):
                    d = [diff(v, c) for v in range(VARS)]
                    source = d[1][0] + d[2][1] + centre[2][c] * ir + rot(3, c) * mr
                    extra = [source, d[4][0], d[4][1], rot(4, c) * mr, source]
                    for v in range(VARS):
                        residual = omega * rot(v, c) + m * d[v][0] + extra[v]
                        value = centre[v][c] - dt * (residual - DAMPING * d[v][2])
                        T[t + 1, l, base + v * 2 + c, pl.ds(r0, 8), :] = value
            return carry

        lax.fori_loop(lo, hi, layer_body, 0)

    def pick(i, values):
        chosen = 0
        for j, value in enumerate(values):
            if value:
                chosen = chosen + jnp.where(i == j, value, 0)
        return chosen

    @pl.loop(0, len(STEPS))
    def _(i):
        t = pick(i, [s[0] for s in STEPS])
        k = pick(i, [s[1] for s in STEPS])

        @pl.when(t == 0)
        def _():
            fetched(k)

        @pl.when(i == 0)
        def _():
            arrived(coef.at[:, pl.ds(theirs, layers)], coef_recv)

        @pl.when(t > 0)
        def _():
            radial_all(t - 1, k, "wait_recv")
            z_all(t - 1, k, "wait_recv")
            update(t - 1, k, jnp.where(front, t + 1, 1), top)

        @pl.when(t < ITERS)
        def _():
            z_all(t, k, "start")
            radial_all(t, k, "start")

        @pl.when((t == ITERS) & (ax != 1))
        def _():
            give_back(k).start()

        @pl.when((t == ITERS) & (ax != 0))
        def _():
            keep(k).start()

        pl.when(i == 1)(sum_rad)
        pl.when(i == 4)(sum_pair)
        pl.when((i == 8) & front)(inlet)

    @pl.when(front)
    def _():
        inlet_arrived()

        @pl.loop(0, ITERS * HARM)
        def _(i):
            t = i // HARM
            k = lax.rem(i, HARM)
            radial_late(t, k, "wait_recv")
            update(t, k, 1, t + 2)
            radial_late(t + 1, k, "start")

            @pl.when((t == ITERS - 1) & (ax == 1))
            def _():
                give_back(k).start()

            @pl.when((t == ITERS - 1) & (ax == 0))
            def _():
                keep(k).start()

    give_coef().wait_send()

    @pl.loop(0, HARM)
    def _(k):
        fetch(k).wait_send()
        given(k)
        give_back(k).wait_send()
        keep(k).wait()

    @pl.loop(0, ITERS * HARM)
    def _(i):
        t = i // HARM
        k = lax.rem(i, HARM)
        z_all(t, k, "wait_send")
        radial_all(t, k, "wait_send")
        pl.when(front)(lambda: radial_late(t, k, "wait_send"))

    for d in range(1, n_rad):
        scatter(d).wait_send()
    to_mate().wait_send()
    pl.when(pair > 0)(lambda: to_front().wait_send())
    pl.when(front)(lambda: hand_out_all("wait_send"))


def on_device(
    n_ax, n_rad,
    face_data, face_station, face_counts, mode_slots, radial_proj, radial_modes,
    duct_field, mean_mach, pseudo_step,
):
    layers, rows = duct_field.shape[:2]
    slots = face_station.shape[0]
    valid = jnp.arange(slots) < face_counts[0]
    orders = mode_slots - NMODE // 2
    frequency_order = jnp.arange(1, HARM + 1)
    moments = jnp.arange(SAMPLE_MOMENTS)
    turns = (frequency_order[:, None] * moments[None, :] % SAMPLE_MOMENTS).astype(
        jnp.float32
    ) * (2.0 * math.pi / SAMPLE_MOMENTS)
    twiddle = jnp.stack([jnp.cos(turns), -jnp.sin(turns)], axis=0) * (2.0 / SAMPLE_MOMENTS)
    width = face_data.shape[3]
    weights = (
        twiddle[:, :, None, :, None] * radial_proj[None, None, :, None, :]
    ).reshape(2 * HARM * NRM, SAMPLE_MOMENTS * width)
    face = jnp.transpose(face_data, (1, 2, 3, 0))
    phase = jnp.mod(face_station[:, None] * orders[None, :], NTH).astype(jnp.float32) * (
        2.0 * math.pi / NTH
    )
    cosine = jnp.where(valid[:, None], jnp.cos(phase), 0.0)
    sine = jnp.where(valid[:, None], jnp.sin(phase), 0.0)

    radial_start = lax.axis_index("rad") * rows
    global_rows = (radial_start + jnp.arange(rows)).astype(jnp.float32)
    inv_radius = 1.0 / (NRD + global_rows + 0.5)
    modes = orders.astype(jnp.float32).reshape(2, 1, 128)
    invr = jnp.broadcast_to(inv_radius[:, None], (rows, 128))
    mode_r = modes * inv_radius[None, :, None]
    coef = jnp.broadcast_to(
        jnp.stack([mean_mach, pseudo_step])[..., None], (2, layers, rows, HALF)
    )
    x = jnp.transpose(duct_field.reshape(layers, rows, PLANES, NMODE), (0, 2, 1, 3))

    share = 2 * SLOTS // n_rad
    half_share = share // 2
    pairs = n_ax // 2
    deep = 2 * layers
    vmem = pl.BlockSpec(memory_space=pltpu.VMEM)
    anywhere = pl.BlockSpec(memory_space=pl.ANY)
    dma = pltpu.SemaphoreType.DMA
    per_side = dma((ITERS, HARM, 2))
    out = pl.pallas_call(
        functools.partial(kernel, n_ax, n_rad, layers, rows),
        out_shape=jax.ShapeDtypeStruct((layers, PLANES, rows, NMODE), jnp.float32),
        in_specs=[anywhere] + [vmem] * 8,
        out_specs=anywhere,
        scratch_shapes=[
            pltpu.VMEM((ITERS + 1, deep + 2, PLANES, rows + 2 * PAD, HALF), jnp.float32),
            pltpu.VMEM((2, deep + 2, rows, HALF), jnp.float32),
            pltpu.VMEM((2 * SLOTS, NRM, HALF), jnp.float32),
            pltpu.VMEM((n_rad - 1, share, NRM, HALF), jnp.float32),
            pltpu.VMEM((share, NRM, HALF), jnp.float32),
            pltpu.VMEM((half_share, NRM, HALF), jnp.float32),
            pltpu.VMEM((1, half_share, NRM, HALF), jnp.float32),
            pltpu.VMEM((pairs - 1, half_share, NRM, HALF), jnp.float32),
            pltpu.VMEM((n_rad, half_share, rows, HALF), jnp.float32),
            pltpu.VMEM((SLOTS, rows, HALF), jnp.float32),
            dma, dma((HARM,)), dma, dma, dma,
            dma((HARM,)), dma((HARM,)), dma((HARM,)), dma((HARM,)),
            per_side, per_side, per_side, per_side, per_side, per_side,
            dma((n_rad - 1,)), dma((n_rad - 1,)),
            dma, dma, dma, dma((pairs - 1,)),
            dma((n_rad,)), dma((n_rad,)),
        ],
        compiler_params=pltpu.CompilerParams(
            collective_id=0, has_side_effects=True, vmem_limit_bytes=60 * 1024 * 1024
        ),
    )(x, face, weights, cosine, sine, radial_modes, coef, invr, mode_r)
    return jnp.transpose(out, (0, 2, 1, 3)).reshape(duct_field.shape)


def solution(mesh):
    in_specs = (
        P("ax", None, None, "rad"),
        P("ax"),
        P("ax"),
        P(),
        P(None, "rad"),
        P(),
        P("ax", "rad", None, None, None, None),
        P("ax", "rad"),
        P("ax", "rad"),
    )
    out_specs = P("ax", "rad", None, None, None, None)
    return jax.shard_map(
        functools.partial(on_device, mesh.shape["ax"], mesh.shape["rad"]),
        mesh=mesh, in_specs=in_specs, out_specs=out_specs, check_vma=False,
    )
```

```python
import functools
import math

import jax
import jax.numpy as jnp
from jax import lax
from jax.experimental import pallas as pl
from jax.experimental.pallas import tpu as pltpu
from jax.sharding import PartitionSpec as P

NTH = 512
SAMPLE_MOMENTS = 7
HARM = 3
NMODE = 256
NRM = 32
NRD = 64
ITERS = 3
VARS = 5

OMEGA_STEP = 0.35
DAMPING = 0.25

MESH = pl.DeviceIdType.MESH
GROUP = VARS * 2
PLANES = HARM * GROUP
PAD = 8
HALF = 128
SLOTS = 32
STEPS = (
    (0, 0), (0, 1), (1, 0), (2, 0), (0, 2), (1, 1),
    (3, 0), (2, 1), (1, 2), (3, 1), (2, 2), (3, 2),
)


def dot_nn(a, b):
    return lax.dot_general(
        a, b, (((1,), (0,)), ((), ())),
        precision=lax.Precision.HIGHEST, preferred_element_type=jnp.float32,
    )


def kernel(
    n_ax, n_rad, layers, rows,
    x_hbm, face, weights, cosine, sine, shapes, coef_in, invr, mode_r,
    out,
    T, D, land, coef, part, a_recv, total, y_recv, merged, c_recv, bound, ghost,
    load_sem, out_sem, coef_load, coef_send, coef_recv,
    in_send, in_recv, back_send, back_recv,
    z_send, z_recv, rad_send, rad_recv, late_send, late_recv, put_sem,
    a_send, a_sem, y_send, y_sem, c_send, c_sem, d_send, d_sem,
):
    ax = lax.axis_index("ax")
    rad = lax.axis_index("rad")
    side_y = lax.rem(ax, 2)
    pair = ax // 2
    mate = ax + 1 - 2 * side_y
    pairs = n_ax // 2
    deep = 2 * layers
    top = deep + 1
    own = pl.ds(PAD, rows)
    share = 2 * SLOTS // n_rad
    half_share = share // 2
    mine = 1 + side_y * layers
    theirs = 1 + (1 - side_y) * layers
    my_lanes = pl.ds(pl.multiple_of(side_y * HALF, HALF), HALF)
    their_lanes = pl.ds(pl.multiple_of((1 - side_y) * HALF, HALF), HALF)
    front = pair == 0

    barrier = pltpu.get_barrier_semaphore()

    def greet(**where):
        pl.semaphore_signal(barrier, inc=1, device_id=where, device_id_type=MESH)

    greet(ax=mate)
    for d in range(1, n_rad):
        greet(rad=lax.rem(rad + d, n_rad))

    @pl.when(front)
    def _():
        for i in range(1, pairs):
            greet(ax=ax + 2 * i)
        for d in range(1, n_rad):
            pl.semaphore_signal(
                barrier, inc=1,
                device_id=(mate, lax.rem(rad + d, n_rad)), device_id_type=MESH,
            )

    @pl.when(pair > 0)
    def _():
        greet(ax=side_y)

    @pl.when(pair > 1)
    def _():
        greet(ax=ax - 2)

    @pl.when((pair > 0) & (pair < pairs - 1))
    def _():
        greet(ax=ax + 2)

    count = (
        1 + (n_rad - 1)
        + jnp.where(front, pairs - 1 + n_rad - 1, 1)
        + jnp.where(pair > 1, 1, 0)
        + jnp.where((pair > 0) & (pair < pairs - 1), 1, 0)
    )
    pl.semaphore_wait(barrier, count)

    def group(k):
        return pl.ds(k * GROUP, GROUP)

    def remote(src, dst, send, recv, **where):
        return pltpu.make_async_remote_copy(
            src_ref=src, dst_ref=dst, send_sem=send, recv_sem=recv,
            device_id=where, device_id_type=MESH,
        )

    def arrived(ref, sem):
        pltpu.make_async_copy(ref, ref, sem).wait()

    def fetch(k):
        return remote(
            x_hbm.at[:, group(k), :, their_lanes],
            T.at[0, pl.ds(mine, layers), group(k), own],
            in_send.at[k], in_recv.at[k], ax=mate,
        )

    def fetched(k):
        arrived(T.at[0, pl.ds(theirs, layers), group(k), own], in_recv.at[k])

    def give_back(k):
        return remote(
            T.at[ITERS, pl.ds(theirs, layers), group(k), own],
            land.at[:, group(k)],
            back_send.at[k], back_recv.at[k], ax=mate,
        )

    def given(k):
        arrived(land.at[:, group(k)], back_recv.at[k])

    def along_z(t, k, side):
        return remote(
            T.at[t, deep if side == 0 else 1, group(k), own],
            T.at[t, 0 if side == 0 else top, group(k), own],
            z_send.at[t, k, side], z_recv.at[t, k, side],
            ax=ax + 2 if side == 0 else ax - 2,
        )

    def radial(t, k, side):
        first = rows - PAD if side == 0 else 0
        layers_all = pl.ds(1, deep)
        return remote(
            T.at[t, layers_all, group(k), pl.ds(PAD + first, PAD)],
            T.at[t, layers_all, group(k), pl.ds(0 if side == 0 else PAD + rows, PAD)],
            rad_send.at[t, k, side], rad_recv.at[t, k, side],
            rad=rad + 1 if side == 0 else rad - 1,
        )

    def radial_inlet(t, hs, side):
        first = rows - PAD if side == 0 else 0
        return remote(
            D.at[hs, t, pl.ds(1, t), :, pl.ds(PAD + first, PAD)],
            D.at[hs, t, pl.ds(1, t), :, pl.ds(0 if side == 0 else PAD + rows, PAD)],
            late_send.at[t, hs, side], late_recv.at[t, hs, side],
            rad=rad + 1 if side == 0 else rad - 1,
        )

    can_send = {
        ("z", 0): pair < pairs - 1, ("z", 1): pair > 0,
        ("rad", 0): rad < n_rad - 1, ("rad", 1): rad > 0,
    }
    can_recv = {
        ("z", 0): pair > 0, ("z", 1): pair < pairs - 1,
        ("rad", 0): rad > 0, ("rad", 1): rad < n_rad - 1,
    }

    def z_all(t, k, what):
        table = can_recv if what == "wait_recv" else can_send
        for side in (0, 1):
            pl.when(table["z", side])(
                lambda side=side: getattr(along_z(t, k, side), what)()
            )

    def radial_all(t, k, what):
        table = can_recv if what == "wait_recv" else can_send
        for side in (0, 1):
            pl.when(table["rad", side])(
                lambda side=side: getattr(radial(t, k, side), what)()
            )

    def radial_inlet_all(t, what):
        table = can_recv if what == "wait_recv" else can_send
        for hs in (0, 1):
            for side in (0, 1):
                pl.when(table["rad", side])(
                    lambda hs=hs, side=side: getattr(radial_inlet(t, hs, side), what)()
                )

    def give_coef():
        return remote(coef_in, coef.at[:, pl.ds(mine, layers)], coef_send, coef_recv, ax=mate)

    fetch(0).start()
    give_coef().start()
    for k in range(1, HARM):
        fetch(k).start()
    load = pltpu.make_async_copy(
        x_hbm.at[:, :, :, my_lanes], T.at[0, pl.ds(mine, layers), :, own], load_sem
    )
    load.start()
    keep_coef = pltpu.make_async_copy(coef_in, coef.at[:, pl.ds(mine, layers)], coef_load)
    keep_coef.start()

    zero_rows = jnp.zeros((PAD, 128), jnp.float32)

    @pl.when(pair == pairs - 1)
    def _():
        @pl.loop(0, PLANES)
        def _(q):
            for t in range(ITERS):
                T[t, top, q, own, :] = jnp.zeros((rows, 128), jnp.float32)

    @pl.when(front)
    def _():
        @pl.loop(0, PLANES)
        def _(q):
            for t in range(ITERS):
                T[t, 0, q, own, :] = jnp.zeros((rows, 128), jnp.float32)

    @pl.when(ax == 0)
    def _():
        @pl.loop(0, PLANES)
        def _(q):
            for hs in range(2):
                for t in range(ITERS):
                    for l in (t + 1, t + 2):
                        D[hs, t, l, q] = jnp.zeros((rows + 2 * PAD, 128), jnp.float32)
                    for l in range(1, t + 1):
                        D[hs, t, l, q, pl.ds(0, PAD), :] = zero_rows
                        D[hs, t, l, q, pl.ds(PAD + rows, PAD), :] = zero_rows

    for edge, start in ((rad == 0, 0), (rad == n_rad - 1, PAD + rows)):
        @pl.when(edge)
        def _(start=start):
            @pl.loop(0, PLANES)
            def _(q):
                for t in range(ITERS):
                    for l in range(1, top):
                        T[t, l, q, pl.ds(start, PAD), :] = zero_rows

    for sh in range(2):
        for q in range(PLANES, SLOTS):
            part[sh * SLOTS + q] = jnp.zeros((NRM, HALF), jnp.float32)
    for v in range(VARS):
        spectra = dot_nn(
            weights[...], jnp.concatenate([face[t, v] for t in range(SAMPLE_MOMENTS)], axis=0)
        )
        half = HARM * NRM
        y0, y1 = spectra[:half], spectra[half:]
        real = dot_nn(y0, cosine[...]) + dot_nn(y1, sine[...])
        imag = dot_nn(y1, cosine[...]) - dot_nn(y0, sine[...])
        for c, value in ((0, real), (1, imag)):
            for k in range(HARM):
                for sh in range(2):
                    part[sh * SLOTS + k * GROUP + v * 2 + c] = value[
                        k * NRM:(k + 1) * NRM, sh * HALF:(sh + 1) * HALF
                    ]

    def scatter(d):
        peer = lax.rem(rad + d, n_rad)
        return remote(
            part.at[pl.ds(peer * share, share)], a_recv.at[d - 1],
            a_send.at[d - 1], a_sem.at[d - 1], rad=peer,
        )

    for d in range(1, n_rad):
        scatter(d).start()

    load.wait()
    keep_coef.wait()

    def keep(kk):
        return pltpu.make_async_copy(
            T.at[ITERS, pl.ds(mine, layers), group(kk), own],
            out.at[:, group(kk), :, my_lanes],
            out_sem.at[kk],
        )

    def to_mate():
        return remote(
            total.at[pl.ds((1 - side_y) * half_share, half_share)], y_recv,
            y_send, y_sem, ax=mate,
        )

    def to_front():
        return remote(merged.at[0], c_recv.at[pair - 1], c_send, c_sem.at[pair - 1], ax=side_y)

    def hand_out(r):
        return pltpu.make_async_remote_copy(
            src_ref=bound.at[r],
            dst_ref=ghost.at[pl.ds(rad * share + side_y * half_share, half_share)],
            send_sem=d_send.at[r],
            recv_sem=d_sem.at[rad * 2 + side_y],
            device_id=(0, r),
            device_id_type=MESH,
        )

    def hand_out_all(what):
        for r in range(n_rad):
            pl.when(jnp.logical_not((ax == 0) & (rad == r)))(
                lambda r=r: getattr(hand_out(r), what)()
            )

    def sum_rad():
        for d in range(1, n_rad):
            scatter(d).wait_recv()

        @pl.loop(0, share)
        def _(q):
            acc = part[rad * share + q]
            for d in range(n_rad - 1):
                acc = acc + a_recv[d, q]
            total[q] = acc

        to_mate().start()

    def sum_pair():
        arrived(y_recv, y_sem)

        @pl.loop(0, half_share)
        def _(q):
            merged[0, q] = total[side_y * half_share + q] + y_recv[q]

        pl.when(pair > 0)(lambda: to_front().start())

    def inlet():
        for i in range(pairs - 1):
            arrived(c_recv.at[i], c_sem.at[i])

        @pl.loop(0, half_share)
        def _(q):
            acc = merged[0, q]
            for i in range(pairs - 1):
                acc = acc + c_recv[i, q]
            value = dot_nn(shapes[...], acc)
            for r in range(n_rad):
                bound[r, q] = value[r * rows:(r + 1) * rows]

        hand_out_all("start")

        @pl.when(ax == 0)
        def _():
            @pl.loop(0, half_share)
            def _(q):
                ghost[rad * share + q] = bound[rad, q]

    def inlet_arrived():
        for i in range(n_rad):
            for sy in range(2):
                pl.when(jnp.logical_not((rad == i) & (sy == 0)))(
                    lambda i=i, sy=sy: arrived(
                        ghost.at[pl.ds(i * share + sy * half_share, half_share)],
                        d_sem.at[i * 2 + sy],
                    )
                )

        @pl.loop(0, PLANES)
        def _(q):
            for hs in range(2):
                value = ghost[hs * SLOTS + q]
                for t in range(ITERS):
                    D[hs, t, 0, q, own, :] = value

    def update(buf, where, sh, t, k, lo, hi):
        omega = OMEGA_STEP * (k + 1).astype(jnp.float32)
        base = k * GROUP

        def layer_body(l, carry):
            for h in range(rows // 8):
                r0 = PAD + 8 * h
                here = pl.ds(8 * h, 8)
                m = coef[0, l, here, :]
                dt = coef[1, l, here, :]
                ir = invr[here, :]
                mr = mode_r[sh, here, :]

                def get(v, c, dl=0, dr=0):
                    return buf[(*where, t, l + dl, base + v * 2 + c, pl.ds(r0 + dr, 8), slice(None))]

                centre = [[get(v, c) for c in (0, 1)] for v in range(VARS)]

                def rot(v, c):
                    return -centre[v][1] if c == 0 else centre[v][0]

                def diff(v, c):
                    up, dn = get(v, c, 1), get(v, c, -1)
                    rt, lf = get(v, c, 0, 1), get(v, c, 0, -1)
                    along = (up - dn) * 0.5
                    across = (rt - lf) * 0.5
                    return along, across, (up + dn) + (rt + lf) - 4.0 * centre[v][c]

                for c in (0, 1):
                    d = [diff(v, c) for v in range(VARS)]
                    source = d[1][0] + d[2][1] + centre[2][c] * ir + rot(3, c) * mr
                    extra = [source, d[4][0], d[4][1], rot(4, c) * mr, source]
                    for v in range(VARS):
                        residual = omega * rot(v, c) + m * d[v][0] + extra[v]
                        value = centre[v][c] - dt * (residual - DAMPING * d[v][2])
                        buf[(*where, t + 1, l, base + v * 2 + c, pl.ds(r0, 8), slice(None))] = value
            return carry

        lax.fori_loop(lo, hi, layer_body, 0)

    def pick(i, values):
        chosen = 0
        for j, value in enumerate(values):
            if value:
                chosen = chosen + jnp.where(i == j, value, 0)
        return chosen

    @pl.loop(0, len(STEPS))
    def _(i):
        t = pick(i, [s[0] for s in STEPS])
        k = pick(i, [s[1] for s in STEPS])

        @pl.when(t == 0)
        def _():
            fetched(k)

        @pl.when(i == 0)
        def _():
            arrived(coef.at[:, pl.ds(theirs, layers)], coef_recv)

        @pl.when(t > 0)
        def _():
            radial_all(t - 1, k, "wait_recv")
            z_all(t - 1, k, "wait_recv")
            update(T, (), side_y, t - 1, k, 1, top)

        @pl.when(t < ITERS)
        def _():
            z_all(t, k, "start")
            radial_all(t, k, "start")

        @pl.when(t == ITERS)
        def _():
            give_back(k).start()

        @pl.when((t == ITERS) & (ax != 0))
        def _():
            keep(k).start()

        pl.when(i == 1)(sum_rad)
        pl.when(i == 4)(sum_pair)
        pl.when((i == 8) & front)(inlet)

    def put(k):
        return pltpu.make_async_copy(
            land.at[:, group(k)], out.at[:, group(k), :, their_lanes], put_sem.at[k]
        )

    @pl.when(ax == 0)
    def _():
        inlet_arrived()
        for t in range(ITERS):
            if t > 0:
                radial_inlet_all(t, "wait_recv")

            @pl.loop(0, 2 * HARM)
            def _(i, t=t):
                hs = i // HARM
                update(D, (hs,), hs, t, lax.rem(i, HARM), 1, t + 2)

            if t < ITERS - 1:
                radial_inlet_all(t + 1, "start")

        @pl.loop(0, HARM)
        def _(k):
            @pl.loop(0, GROUP)
            def _(j):
                q = k * GROUP + j
                for l in range(1, ITERS + 1):
                    T[ITERS, l, q, own, :] = T[ITERS, l, q, own, :] + D[0, ITERS, l, q, own, :]

            keep(k).start()

    @pl.loop(0, HARM)
    def _(k):
        given(k)

        @pl.when(ax == 0)
        def _():
            @pl.loop(0, GROUP)
            def _(j):
                q = k * GROUP + j
                for l in range(1, ITERS + 1):
                    land[l - 1, q] = land[l - 1, q] + D[1, ITERS, l, q, own, :]

        put(k).start()

    give_coef().wait_send()

    @pl.loop(0, HARM)
    def _(k):
        fetch(k).wait_send()
        give_back(k).wait_send()
        put(k).wait()
        keep(k).wait()

    @pl.loop(0, ITERS * HARM)
    def _(i):
        t = i // HARM
        k = lax.rem(i, HARM)
        z_all(t, k, "wait_send")
        radial_all(t, k, "wait_send")

    for d in range(1, n_rad):
        scatter(d).wait_send()
    to_mate().wait_send()
    pl.when(pair > 0)(lambda: to_front().wait_send())
    pl.when(front)(lambda: hand_out_all("wait_send"))

    @pl.when(ax == 0)
    def _():
        for t in range(1, ITERS):
            radial_inlet_all(t, "wait_send")


def on_device(
    n_ax, n_rad,
    face_data, face_station, face_counts, mode_slots, radial_proj, radial_modes,
    duct_field, mean_mach, pseudo_step,
):
    layers, rows = duct_field.shape[:2]
    slots = face_station.shape[0]
    valid = jnp.arange(slots) < face_counts[0]
    orders = mode_slots - NMODE // 2
    frequency_order = jnp.arange(1, HARM + 1)
    moments = jnp.arange(SAMPLE_MOMENTS)
    turns = (frequency_order[:, None] * moments[None, :] % SAMPLE_MOMENTS).astype(
        jnp.float32
    ) * (2.0 * math.pi / SAMPLE_MOMENTS)
    twiddle = jnp.stack([jnp.cos(turns), -jnp.sin(turns)], axis=0) * (2.0 / SAMPLE_MOMENTS)
    width = face_data.shape[3]
    weights = (
        twiddle[:, :, None, :, None] * radial_proj[None, None, :, None, :]
    ).reshape(2 * HARM * NRM, SAMPLE_MOMENTS * width)
    face = jnp.transpose(face_data, (1, 2, 3, 0))
    phase = jnp.mod(face_station[:, None] * orders[None, :], NTH).astype(jnp.float32) * (
        2.0 * math.pi / NTH
    )
    cosine = jnp.where(valid[:, None], jnp.cos(phase), 0.0)
    sine = jnp.where(valid[:, None], jnp.sin(phase), 0.0)

    radial_start = lax.axis_index("rad") * rows
    global_rows = (radial_start + jnp.arange(rows)).astype(jnp.float32)
    inv_radius = 1.0 / (NRD + global_rows + 0.5)
    modes = orders.astype(jnp.float32).reshape(2, 1, 128)
    invr = jnp.broadcast_to(inv_radius[:, None], (rows, 128))
    mode_r = modes * inv_radius[None, :, None]
    coef = jnp.broadcast_to(
        jnp.stack([mean_mach, pseudo_step])[..., None], (2, layers, rows, HALF)
    )
    x = jnp.transpose(duct_field.reshape(layers, rows, PLANES, NMODE), (0, 2, 1, 3))

    share = 2 * SLOTS // n_rad
    half_share = share // 2
    pairs = n_ax // 2
    deep = 2 * layers
    vmem = pl.BlockSpec(memory_space=pltpu.VMEM)
    anywhere = pl.BlockSpec(memory_space=pl.ANY)
    dma = pltpu.SemaphoreType.DMA
    per_side = dma((ITERS, HARM, 2))
    out = pl.pallas_call(
        functools.partial(kernel, n_ax, n_rad, layers, rows),
        out_shape=jax.ShapeDtypeStruct((layers, PLANES, rows, NMODE), jnp.float32),
        in_specs=[anywhere] + [vmem] * 8,
        out_specs=anywhere,
        scratch_shapes=[
            pltpu.VMEM((ITERS + 1, deep + 2, PLANES, rows + 2 * PAD, HALF), jnp.float32),
            pltpu.VMEM((2, ITERS + 1, ITERS + 2, PLANES, rows + 2 * PAD, HALF), jnp.float32),
            pltpu.VMEM((layers, PLANES, rows, HALF), jnp.float32),
            pltpu.VMEM((2, deep + 2, rows, HALF), jnp.float32),
            pltpu.VMEM((2 * SLOTS, NRM, HALF), jnp.float32),
            pltpu.VMEM((n_rad - 1, share, NRM, HALF), jnp.float32),
            pltpu.VMEM((share, NRM, HALF), jnp.float32),
            pltpu.VMEM((half_share, NRM, HALF), jnp.float32),
            pltpu.VMEM((1, half_share, NRM, HALF), jnp.float32),
            pltpu.VMEM((pairs - 1, half_share, NRM, HALF), jnp.float32),
            pltpu.VMEM((n_rad, half_share, rows, HALF), jnp.float32),
            pltpu.VMEM((2 * SLOTS, rows, HALF), jnp.float32),
            dma, dma((HARM,)), dma, dma, dma,
            dma((HARM,)), dma((HARM,)), dma((HARM,)), dma((HARM,)),
            per_side, per_side, per_side, per_side, per_side, per_side, dma((HARM,)),
            dma((n_rad - 1,)), dma((n_rad - 1,)),
            dma, dma, dma, dma((pairs - 1,)),
            dma((n_rad,)), dma((2 * n_rad,)),
        ],
        compiler_params=pltpu.CompilerParams(
            collective_id=0, has_side_effects=True, vmem_limit_bytes=60 * 1024 * 1024
        ),
    )(x, face, weights, cosine, sine, radial_modes, coef, invr, mode_r)
    return jnp.transpose(out, (0, 2, 1, 3)).reshape(duct_field.shape)


def solution(mesh):
    in_specs = (
        P("ax", None, None, "rad"),
        P("ax"),
        P("ax"),
        P(),
        P(None, "rad"),
        P(),
        P("ax", "rad", None, None, None, None),
        P("ax", "rad"),
        P("ax", "rad"),
    )
    out_specs = P("ax", "rad", None, None, None, None)
    return jax.shard_map(
        functools.partial(on_device, mesh.shape["ax"], mesh.shape["rad"]),
        mesh=mesh, in_specs=in_specs, out_specs=out_specs, check_vma=False,
    )
```
